32 devices in a mesh: gx: 4 (over y, x), gy: 4 (over z), gz: 2 (over core).
Axes of the slice: x: 2, y: 2, z: 4, core: 2. Of those that a mesh axis runs over, the one named last changes fastest.
Arguments:
- viscosity: float32 [128, 64, 256], P('gx', 'gy', 'gz'), may hold values from 0.001 to 1000
- force: float32 [3, 128, 64, 256], P(None, 'gx', 'gy', 'gz'), may hold values from -6 to 6
Outputs:
- solution: float32 [4, 128, 64, 256], P(None, 'gx', 'gy', 'gz')
- residual: float32 [4, 128, 64, 256], P(None, 'gx', 'gy', 'gz')
The draws below stay inside these ranges and needn't reach their ends.
All inputs are finite; a program needn't handle non-finite values.
Results may differ from the reference program's by a relative error of at most 0.0003.
Values sent between devices are 32-bit elements; how exact they have to be, the bound alone decides.
A program may use at most 128 MiB of HBM per device.

```python
import math
import jax
import jax.numpy as jnp
from jax import lax

CHEB = 4
ITERS = 2
NX = 128
NY = 64
NZ = 256


def steps_of(rng, dims, pieces, low, largest):
    level = 1.0
    for dim, shards_of in pieces:
        draws = jax.random.uniform(jax.random.fold_in(jax.random.fold_in(rng, 6), dim), (shards_of,), jnp.float32, low / len(pieces), largest / len(pieces))
        level = level * jnp.repeat(jnp.exp(draws), dims[dim] // shards_of).reshape((-1,) + (1,) * (len(dims) - 1 - dim))
    return level


def scatter_about(own_key, dims, deviation, bound, cuts=(), kind=jnp.bfloat16):
    values = deviation * jax.random.normal(own_key, dims, jnp.float32)
    if cuts:
        values = values * steps_of(own_key, dims, cuts, -0.22, 0.18)
    return jnp.clip(values, -bound, bound).astype(kind)


def setup_inputs(seed: int = 0) -> dict:
    splits = jax.random.split(jax.random.key(seed), 3)
    viscosity = jnp.clip(jnp.exp(math.log(1000.0) - 13.815511 * jax.random.uniform(splits[0], (NX, NY, NZ), jnp.float32) ** steps_of(splits[0], (NX, NY, NZ), ((0, 4), (1, 4), (2, 2)), -0.2, 0.2)), 0.001, 1000.0)
    force = scatter_about(splits[1], (3, NX, NY, NZ), 1.0, 6.0, ((1, 4), (2, 4), (3, 2)), jnp.float32)
    return dict(viscosity=viscosity, force=force)


low_edge = 0.25
high_edge = 2.0

def coefficients(padded_eta):
    middle = padded_eta[1:-1, 1:-1, 1:-1]
    x_plus = 0.5 * (middle + padded_eta[2:, 1:-1, 1:-1])
    x_minus = 0.5 * (middle + padded_eta[:-2, 1:-1, 1:-1])
    y_plus = 0.5 * (middle + padded_eta[1:-1, 2:, 1:-1])
    y_minus = 0.5 * (middle + padded_eta[1:-1, :-2, 1:-1])
    z_plus = 0.5 * (middle + padded_eta[1:-1, 1:-1, 2:])
    z_minus = 0.5 * (middle + padded_eta[1:-1, 1:-1, :-2])
    diagonal = x_plus + x_minus + y_plus + y_minus + z_plus + z_minus
    return (x_plus, x_minus, y_plus, y_minus, z_plus, z_minus, diagonal)

def viscous(padded, stencil):
    x_plus, x_minus, y_plus, y_minus, z_plus, z_minus, diagonal = stencil
    result = diagonal * padded[:, 1:-1, 1:-1, 1:-1]
    result = result - x_plus * padded[:, 2:, 1:-1, 1:-1] - x_minus * padded[:, :-2, 1:-1, 1:-1]
    result = result - y_plus * padded[:, 1:-1, 2:, 1:-1] - y_minus * padded[:, 1:-1, :-2, 1:-1]
    result = result - z_plus * padded[:, 1:-1, 1:-1, 2:] - z_minus * padded[:, 1:-1, 1:-1, :-2]
    return result

def stokes(padded, stencil):
    velocity = padded[:3]
    pressure = padded[3]
    gradient = jnp.stack([0.5 * (pressure[2:, 1:-1, 1:-1] - pressure[:-2, 1:-1, 1:-1]), 0.5 * (pressure[1:-1, 2:, 1:-1] - pressure[1:-1, :-2, 1:-1]), 0.5 * (pressure[1:-1, 1:-1, 2:] - pressure[1:-1, 1:-1, :-2])])
    divergence = -0.5 * (velocity[0, 2:, 1:-1, 1:-1] - velocity[0, :-2, 1:-1, 1:-1] + (velocity[1, 1:-1, 2:, 1:-1] - velocity[1, 1:-1, :-2, 1:-1]) + (velocity[2, 1:-1, 1:-1, 2:] - velocity[2, 1:-1, 1:-1, :-2]))
    return jnp.concatenate([viscous(velocity, stencil) + gradient, divergence[None]], axis=0)

def pad_cells(field):
    return jnp.pad(field, ((0, 0), (1, 1), (1, 1), (1, 1)))

def chebyshev(forcing, inverse, apply_block):
    middle = 0.5 * (high_edge + low_edge)
    half_width = 0.5 * (high_edge - low_edge)
    scaled = middle / half_width
    ratio_now = 1.0 / scaled
    update = forcing * inverse / middle
    result = update
    remainder = forcing
    for sweep_at in range(CHEB - 1):
        remainder = remainder - apply_block(update)
        ratio_next = 1.0 / (2.0 * scaled - ratio_now)
        update = ratio_next * ratio_now * update + 2.0 * ratio_next / half_width * remainder * inverse
        result = result + update
        ratio_now = ratio_next
    return result

def least_squares(columns, initial_norm):
    hessen = jnp.stack(columns, axis=1)
    normal = jnp.dot(hessen.T, hessen, precision=lax.Precision.HIGHEST)
    target = initial_norm * hessen[0]
    factor = jnp.linalg.cholesky(normal)
    size_of = len(columns)
    forward = []
    for row_at in range(size_of):
        running = target[row_at]
        for inner_at in range(row_at):
            running = running - factor[row_at, inner_at] * forward[inner_at]
        forward.append(running / factor[row_at, row_at])
    backward = [None] * size_of
    for row_at in reversed(range(size_of)):
        running = forward[row_at]
        for inner_at in range(row_at + 1, size_of):
            running = running - factor[inner_at, row_at] * backward[inner_at]
        backward[row_at] = running / factor[row_at, row_at]
    weights = jnp.stack(backward)
    leading = jnp.zeros((size_of + 1,), jnp.float32).at[0].set(initial_norm)
    misfit = leading - jnp.dot(hessen, weights, precision=lax.Precision.HIGHEST)
    return (backward, misfit)

def reference(viscosity, force):
    stencil = coefficients(jnp.pad(viscosity, 1))
    inverse = 1.0 / stencil[6]

    def velocity_block(update):
        return viscous(pad_cells(update), stencil)
    rhs_full = jnp.concatenate([force, jnp.zeros((1,) + viscosity.shape, jnp.float32)], axis=0)
    initial_norm = jnp.sqrt(jnp.sum(rhs_full * rhs_full))
    krylov = [rhs_full / initial_norm]
    search = []
    columns = []
    for column_at in range(ITERS):
        current = krylov[column_at]
        smoothed = chebyshev(current[:3], inverse, velocity_block)
        direction = jnp.concatenate([smoothed, (viscosity * current[3])[None]], axis=0)
        search.append(direction)
        candidate = stokes(pad_cells(direction), stencil)
        products = jnp.stack([jnp.sum(candidate * vector) for vector in krylov])
        for row_at in range(column_at + 1):
            candidate = candidate - products[row_at] * krylov[row_at]
        length = jnp.sqrt(jnp.sum(candidate * candidate))
        krylov.append(candidate / length)
        columns.append(jnp.concatenate([products, length[None], jnp.zeros((ITERS - 1 - column_at,), jnp.float32)]))
    weights, misfit = least_squares(columns, initial_norm)
    solution = weights[0] * search[0]
    for column_at in range(1, ITERS):
        solution = solution + weights[column_at] * search[column_at]
    residual = misfit[0] * krylov[0]
    for row_at in range(1, ITERS + 1):
        residual = residual + misfit[row_at] * krylov[row_at]
    return (solution, residual)
```

```python
import functools
import jax
import jax.numpy as jnp
from jax import lax
from jax.experimental import pallas as pl
from jax.experimental.pallas import tpu as pltpu
from jax.sharding import PartitionSpec as P

MESH = pl.DeviceIdType.MESH
AXES = ("gx", "gy", "gz")
SWEEPS = 3
LOW, HIGH = 0.25, 2.0
ROUNDS = 9
WIDTHS = (1, 3, 3, 3, 3, 4, 3, 3, 3)
UNROLL = 4


def cheb_constants():
    mid, half = 0.5 * (HIGH + LOW), 0.5 * (HIGH - LOW)
    s = mid / half
    rho = 1.0 / s
    steps = []
    for _ in range(SWEEPS):
        nxt = 1.0 / (2.0 * s - rho)
        steps.append((nxt * rho, 2.0 * nxt / half))
        rho = nxt
    return mid, steps


def kernel(counts, chunks, eta_hbm, force_hbm, sol_hbm, res_hbm,
           e_ref, b_ref, f_ref, cx_ref, cym_ref, cyp_ref, czm_ref, czp_ref, dg_ref, inv_ref,
           r_ref, x_ref, w0_ref, w1_ref, so_ref, ro_ref,
           sy_ref, hy_ref, sz_ref, hz_ref, ar_ref,
           in_sem, out_sem, xs_sem, xr_sem, ys_sem, yr_sem, zs_sem, zr_sem, as_sem, ar_sem):
    X, Y, Z = b_ref.shape[1:]
    mid, steps = cheb_constants()
    me = [lax.axis_index(a) for a in AXES]
    nch = len(chunks)
    order = [0] + ([nch - 1] if nch > 1 else []) + list(range(1, nch - 1))

    load_e = pltpu.make_async_copy(eta_hbm, e_ref.at[0, pl.ds(1, X)], in_sem.at[0])
    load_b = pltpu.make_async_copy(force_hbm, b_ref, in_sem.at[1])
    load_e.start()
    load_b.start()

    def device(dim, index):
        spot = list(me)
        spot[dim] = index
        return tuple(spot)

    barrier = pltpu.get_barrier_semaphore()
    for dim in range(3):
        for off in range(1, counts[dim]):
            pl.semaphore_signal(barrier, inc=1, device_id=device(dim, lax.rem(me[dim] + off, counts[dim])),
                                device_id_type=MESH)

    def field(k):
        return e_ref if k == 0 else f_ref.at[k - 1]

    def target(dim, side):
        return device(dim, me[dim] + (1 if side == 0 else -1))

    def sends(dim, side):
        return me[dim] < counts[dim] - 1 if side == 0 else me[dim] > 0

    def receives(dim, side):
        return me[dim] > 0 if side == 0 else me[dim] < counts[dim] - 1

    def x_copy(k, side):
        n = WIDTHS[k]
        face, halo = (X, 0) if side == 0 else (1, X + 1)
        return pltpu.make_async_remote_copy(
            src_ref=field(k).at[pl.ds(0, n), face], dst_ref=field(k).at[pl.ds(0, n), halo],
            send_sem=xs_sem.at[k, side], recv_sem=xr_sem.at[k, side],
            device_id=target(0, side), device_id_type=MESH)

    def y_copy(k, side, ch):
        n = WIDTHS[k]
        lo, hi = chunks[ch]
        return pltpu.make_async_remote_copy(
            src_ref=sy_ref.at[k, side, pl.ds(0, n), pl.ds(lo, hi - lo)],
            dst_ref=hy_ref.at[k, side, pl.ds(0, n), pl.ds(lo, hi - lo)],
            send_sem=ys_sem.at[k, side, ch], recv_sem=yr_sem.at[k, side, ch],
            device_id=target(1, side), device_id_type=MESH)

    def z_copy(k, side, ch):
        return pltpu.make_async_remote_copy(
            src_ref=sz_ref.at[k, side, ch], dst_ref=hz_ref.at[k, side, ch],
            send_sem=zs_sem.at[k, side, ch], recv_sem=zr_sem.at[k, side, ch],
            device_id=target(2, side), device_id_type=MESH)

    def start_chunk(k, ch):
        for side in (0, 1):
            @pl.when(sends(1, side))
            def _():
                y_copy(k, side, ch).start()
            @pl.when(sends(2, side))
            def _():
                z_copy(k, side, ch).start()
        for side, edge in ((0, nch - 1), (1, 0)):
            if ch == edge:
                @pl.when(sends(0, side))
                def _():
                    x_copy(k, side).start()

    def wait_chunk(k, ch):
        for side in (0, 1):
            @pl.when(receives(1, side))
            def _():
                y_copy(k, side, ch).wait_recv()
            @pl.when(receives(2, side))
            def _():
                z_copy(k, side, ch).wait_recv()
        for side, edge in ((0, 0), (1, nch - 1)):
            if ch == edge:
                @pl.when(receives(0, side))
                def _():
                    x_copy(k, side).wait_recv()

    for side in (0, 1):
        @pl.when(jnp.logical_not(receives(0, side)))
        def _():
            zero = jnp.zeros((Y, Z), jnp.float32)
            for k in range(ROUNDS):
                for c in range(WIDTHS[k]):
                    field(k)[c, 0 if side == 0 else X + 1] = zero
        @pl.when(jnp.logical_not(receives(1, side)))
        def _():
            def body(k, carry):
                hy_ref[k, side] = jnp.zeros(hy_ref.shape[2:], jnp.float32)
                return carry
            lax.fori_loop(0, ROUNDS, body, 0)
        @pl.when(jnp.logical_not(receives(2, side)))
        def _():
            def body(k, carry):
                hz_ref[k, side] = jnp.zeros(hz_ref.shape[2:], jnp.float32)
                return carry
            lax.fori_loop(0, ROUNDS, body, 0)

    row = lax.broadcasted_iota(jnp.int32, (Y, Z), 0)
    lane = lax.broadcasted_iota(jnp.int32, (Y, Z), 1)
    blank = jnp.zeros((Y, Z), jnp.float32)
    first_row, last_row, first_lane, last_lane = row == 0, row == Y - 1, lane == 0, lane == Z - 1

    def neighbours(k, ch, c, x):
        f = field(k)
        u = f[c, x + 1]
        spot = c * X + x
        ym = jnp.where(first_row, hy_ref[k, 0, c, pl.ds(x, 1)], pltpu.roll(u, 1, 0))
        yp = jnp.where(last_row, hy_ref[k, 1, c, pl.ds(x, 1)], pltpu.roll(u, Y - 1, 0))
        zm = jnp.where(first_lane, pltpu.roll(hz_ref[k, 0, ch], lax.rem(Z - spot, Z), 1), pltpu.roll(u, 1, 1))
        zp = jnp.where(last_lane, pltpu.roll(hz_ref[k, 1, ch], Z - 1 - spot, 1), pltpu.roll(u, Z - 1, 1))
        return u, f[c, x], f[c, x + 2], ym, yp, zm, zp

    def put(k, c, x, value, packs, store=True):
        if store:
            field(k)[c, x + 1] = value
        sy_ref[k, 0, c, pl.ds(x, 1)] = value[Y - 1:Y]
        sy_ref[k, 1, c, pl.ds(x, 1)] = value[0:1]
        here = lane == c * X + x
        return (jnp.where(here, jnp.broadcast_to(value[:, Z - 1:Z], (Y, Z)), packs[0]),
                jnp.where(here, jnp.broadcast_to(value[:, 0:1], (Y, Z)), packs[1]))

    def sweep(need, make, body, extra=()):
        for ch in order:
            if need is not None:
                wait_chunk(need, ch)
            lo, hi = chunks[ch]
            def step(x, carry):
                return body(ch, x, carry[0], carry[1])
            packs, extra = lax.fori_loop(lo, hi, step, ((blank, blank), extra), unroll=UNROLL)
            if make is not None:
                sz_ref[make, 0, ch] = packs[0]
                sz_ref[make, 1, ch] = packs[1]
                start_chunk(make, ch)
        return extra

    load_e.wait()
    pl.semaphore_wait(barrier, sum(counts) - 3)
    sweep(None, 0, lambda ch, x, packs, extra: (put(0, 0, x, e_ref[0, x + 1], packs, False), extra))
    load_b.wait()

    def setup(ch, x, packs, extra):
        u, xm, xp, ym, yp, zm, zp = neighbours(0, ch, 0, x)
        cxm, cxp = 0.5 * (u + xm), 0.5 * (u + xp)
        cym, cyp = 0.5 * (u + ym), 0.5 * (u + yp)
        czm, czp = 0.5 * (u + zm), 0.5 * (u + zp)
        cx_ref[x] = cxm
        cx_ref[x + 1] = cxp
        cym_ref[x], cyp_ref[x], czm_ref[x], czp_ref[x] = cym, cyp, czm, czp
        diagonal = cxp + cxm + cyp + cym + czp + czm
        inverse = 1.0 / diagonal
        dg_ref[x] = diagonal
        inv_ref[x] = inverse
        for c in range(3):
            packs = put(1, c, x, b_ref[c, x] * inverse / mid, packs)
        return packs, extra

    sweep(0, 1, setup)

    def viscous(near, coef):
        u, xm, xp, ym, yp, zm, zp = near
        cxm, cxp, cym, cyp, czm, czp, dg = coef
        return dg * u - cxp * xp - cxm * xm - cyp * yp - cym * ym - czp * zp - czm * zm

    def coefs(x):
        return (cx_ref[x], cx_ref[x + 1], cym_ref[x], cyp_ref[x], czm_ref[x], czp_ref[x], dg_ref[x])

    def smooth(base, forcing, at, shift=None):
        keep, gain = steps[at]
        src, dst = base + at, base + at + 1
        last = at == SWEEPS - 1

        def body(ch, x, packs, extra):
            coef, inverse = coefs(x), inv_ref[x]
            for c in range(3):
                near = neighbours(src, ch, c, x)
                r = (forcing[c, x] if at == 0 else r_ref[c, x]) - viscous(near, coef)
                d = keep * near[0] + gain * r * inverse
                total = (near[0] if at == 0 else x_ref[c, x]) + d
                if last:
                    if shift is not None:
                        total = total - shift * f_ref[base - 2, c, x + 1]
                    packs = put(dst, c, x, total, packs)
                else:
                    r_ref[c, x] = r
                    x_ref[c, x] = total
                    packs = put(dst, c, x, d, packs)
            return packs, extra

        sweep(src, dst, body)

    stages = (2, 0, 1)
    starts = [sum(counts[d] for d in stages[:i]) for i in range(3)]

    def ar_copy(which, stage, off):
        dim = stages[stage]
        slot = starts[stage] + me[dim]
        peer = lax.rem(me[dim] + off, counts[dim])
        return pltpu.make_async_remote_copy(
            src_ref=ar_ref.at[which, slot], dst_ref=ar_ref.at[which, slot],
            send_sem=as_sem.at[which, starts[stage] + off], recv_sem=ar_sem.at[which, slot],
            device_id=device(dim, peer), device_id_type=MESH)

    def ar_start(which, stage, tile):
        dim = stages[stage]
        ar_ref[which, starts[stage] + me[dim]] = tile
        for off in range(1, counts[dim]):
            ar_copy(which, stage, off).start()

    def ar_wait(which, stage):
        dim = stages[stage]
        for off in range(1, counts[dim]):
            slot = starts[stage] + lax.rem(me[dim] + off, counts[dim])
            pltpu.make_async_remote_copy(
                src_ref=ar_ref.at[which, slot], dst_ref=ar_ref.at[which, slot],
                send_sem=as_sem.at[which, starts[stage] + off], recv_sem=ar_sem.at[which, slot],
                device_id=device(dim, lax.rem(me[dim] + off, counts[dim])), device_id_type=MESH).wait_recv()
        total = ar_ref[which, starts[stage]]
        for i in range(1, counts[dim]):
            total = total + ar_ref[which, starts[stage] + i]
        return total

    rows8 = lax.broadcasted_iota(jnp.int32, (8, Z), 0)

    def tile_of(sums):
        tile = jnp.zeros((8, Z), jnp.float32)
        for i, s in enumerate(sums):
            tile = jnp.where(rows8 == i, jnp.sum(s, axis=0, keepdims=True), tile)
        return tile

    def totals(tile, n):
        whole = jnp.broadcast_to(jnp.sum(tile, axis=1, keepdims=True), (8, Z))
        return [whole[i:i + 1] for i in range(n)]

    for at in range(SWEEPS):
        smooth(1, b_ref, at)

    def stokes0(ch, x, packs, sums):
        bb, wb, ww = sums
        coef, inverse = coefs(x), inv_ref[x]
        near = [neighbours(4, ch, c, x) for c in range(3)]
        for c in range(3):
            w, b = viscous(near[c], coef), b_ref[c, x]
            bb, wb, ww = bb + b * b, wb + w * b, ww + w * w
            w0_ref[c, x] = w
            packs = put(5, c, x, w * inverse / mid, packs)
        div = -0.5 * (near[0][2] - near[0][1] + (near[1][4] - near[1][3]) + (near[2][6] - near[2][5]))
        ww = ww + div * div
        w0_ref[3, x] = div
        packs = put(5, 3, x, e_ref[0, x + 1] * div, packs)
        return packs, (bb, wb, ww)

    sums = sweep(4, 5, stokes0, (blank, blank, blank))
    ar_start(0, 0, tile_of(sums))

    smooth(5, w0_ref, 0)
    ar_start(0, 1, ar_wait(0, 0))
    smooth(5, w0_ref, 1)
    ar_start(0, 2, ar_wait(0, 1))
    square, wb, ww = totals(ar_wait(0, 2), 3)
    h00 = wb / square
    h10 = jnp.sqrt(ww / square - h00 * h00)
    smooth(5, w0_ref, 2, h00)

    def stokes1(ch, x, packs, sums):
        wb, wu, ww = sums
        coef = coefs(x)
        near = [neighbours(8, ch, c, x) for c in range(3)]
        _, pxm, pxp, pym, pyp, pzm, pzp = neighbours(5, ch, 3, x)
        grads = (0.5 * (pxp - pxm), 0.5 * (pyp - pym), 0.5 * (pzp - pzm))
        for c in range(3):
            w, b = viscous(near[c], coef) + grads[c], b_ref[c, x]
            u = w0_ref[c, x] - h00 * b
            wb, wu, ww = wb + w * b, wu + w * u, ww + w * w
            w1_ref[c, x] = w
        div = -0.5 * (near[0][2] - near[0][1] + (near[1][4] - near[1][3]) + (near[2][6] - near[2][5]))
        wu, ww = wu + div * w0_ref[3, x], ww + div * div
        w1_ref[3, x] = div
        return packs, (wb, wu, ww)

    sums = sweep(8, None, stokes1, (blank, blank, blank))
    ar_start(1, 0, tile_of(sums))
    ar_start(1, 1, ar_wait(1, 0))
    ar_start(1, 2, ar_wait(1, 1))
    wb, wu, ww = totals(ar_wait(1, 2), 3)

    beta = jnp.sqrt(square)
    h01 = wb / (square * h10)
    h11 = wu / (square * h10 * h10)
    h21 = jnp.sqrt(ww / (square * h10 * h10) - h01 * h01 - h11 * h11)
    n00, n01, n11 = h00 * h00 + h10 * h10, h00 * h01 + h10 * h11, h01 * h01 + h11 * h11 + h21 * h21
    l00 = jnp.sqrt(n00)
    l10 = n01 / l00
    l11 = jnp.sqrt(n11 - l10 * l10)
    g0 = beta * h00 / l00
    g1 = (beta * h01 - l10 * g0) / l11
    y1 = g1 / l11
    y0 = (g0 - l10 * y1) / l00
    c0 = beta - (h00 * y0 + h01 * y1)
    c1 = -(h10 * y0 + h11 * y1)
    c2 = -(h21 * y1)
    z0_weight, z1_weight = y0 / beta, y1 / (beta * h10)
    b_weight = (c0 - c2 * h01 / h21) / beta
    u_weight = (c1 - c2 * h11 / h21) / (beta * h10)
    w_weight = c2 / (h21 * beta * h10)

    def out_copies(ch):
        lo, hi = chunks[ch]
        span = pl.ds(lo, hi - lo)
        return (pltpu.make_async_copy(so_ref.at[:, span], sol_hbm.at[:, span], out_sem.at[0, ch]),
                pltpu.make_async_copy(ro_ref.at[:, span], res_hbm.at[:, span], out_sem.at[1, ch]))

    for ch in range(nch):
        def body(x, carry):
            for c in range(3):
                b = b_ref[c, x]
                so_ref[c, x] = z0_weight * f_ref[3, c, x + 1] + z1_weight * f_ref[7, c, x + 1]
                ro_ref[c, x] = b_weight * b + u_weight * (w0_ref[c, x] - h00 * b) + w_weight * w1_ref[c, x]
            so_ref[3, x] = z1_weight * f_ref[4, 3, x + 1]
            ro_ref[3, x] = u_weight * w0_ref[3, x] + w_weight * w1_ref[3, x]
            return carry
        lax.fori_loop(*chunks[ch], body, 0, unroll=UNROLL)
        for copy in out_copies(ch):
            copy.start()

    for side in (0, 1):
        @pl.when(sends(0, side))
        def _():
            for k in range(ROUNDS):
                x_copy(k, side).wait_send()
        @pl.when(sends(1, side))
        def _():
            for k in range(ROUNDS):
                for ch in range(nch):
                    y_copy(k, side, ch).wait_send()
        @pl.when(sends(2, side))
        def _():
            for k in range(ROUNDS):
                for ch in range(nch):
                    z_copy(k, side, ch).wait_send()
    for which in (0, 1):
        for stage in range(3):
            for off in range(1, counts[stages[stage]]):
                ar_copy(which, stage, off).wait_send()
    for ch in range(nch):
        for copy in out_copies(ch):
            copy.wait()


def solution(mesh):
    counts = tuple(mesh.shape[a] for a in AXES)

    def shards(viscosity, force):
        X, Y, Z = viscosity.shape
        assert 4 * X <= Z
        size = 8 if X % 8 == 0 else X
        chunks = tuple((lo, lo + size) for lo in range(0, X, size))
        nch = len(chunks)
        f32 = jnp.float32
        block = pltpu.VMEM((X, Y, Z), f32)
        dma = pltpu.SemaphoreType.DMA
        spots = sum(counts)
        scratch = [
            pltpu.VMEM((1, X + 2, Y, Z), f32), pltpu.VMEM((3, X, Y, Z), f32),
            pltpu.VMEM((ROUNDS - 1, 4, X + 2, Y, Z), f32), pltpu.VMEM((X + 1, Y, Z), f32),
            block, block, block, block, block, block,
            pltpu.VMEM((3, X, Y, Z), f32), pltpu.VMEM((3, X, Y, Z), f32),
            pltpu.VMEM((4, X, Y, Z), f32), pltpu.VMEM((4, X, Y, Z), f32),
            pltpu.VMEM((4, X, Y, Z), f32), pltpu.VMEM((4, X, Y, Z), f32),
            pltpu.VMEM((ROUNDS, 2, 4, X, Z), f32), pltpu.VMEM((ROUNDS, 2, 4, X, Z), f32),
            pltpu.VMEM((ROUNDS, 2, nch, Y, Z), f32), pltpu.VMEM((ROUNDS, 2, nch, Y, Z), f32),
            pltpu.VMEM((2, spots, 8, Z), f32),
            dma((2,)), dma((2, nch)), dma((ROUNDS, 2)), dma((ROUNDS, 2)),
            dma((ROUNDS, 2, nch)), dma((ROUNDS, 2, nch)), dma((ROUNDS, 2, nch)), dma((ROUNDS, 2, nch)),
            dma((2, spots)), dma((2, spots)),
        ]
        anywhere = pl.BlockSpec(memory_space=pl.ANY)
        out = jax.ShapeDtypeStruct((4, X, Y, Z), f32)
        return tuple(pl.pallas_call(
            functools.partial(kernel, counts, chunks),
            out_shape=(out, out),
            in_specs=[anywhere, anywhere],
            out_specs=(anywhere, anywhere),
            scratch_shapes=scratch,
            name="fgmres",
            compiler_params=pltpu.CompilerParams(
                collective_id=0, has_side_effects=True, vmem_limit_bytes=56 * 1024 * 1024),
        )(viscosity, force))

    return jax.shard_map(
        shards,
        mesh=mesh,
        in_specs=(P("gx", "gy", "gz"), P(None, "gx", "gy", "gz")),
        out_specs=(P(None, "gx", "gy", "gz"), P(None, "gx", "gy", "gz")),
        check_vma=False,
    )
```

```python
import functools
import jax
import jax.numpy as jnp
from jax import lax
from jax.experimental import pallas as pl
from jax.experimental.pallas import tpu as pltpu
from jax.sharding import PartitionSpec as P

MESH = pl.DeviceIdType.MESH
AXES = ("gx", "gy", "gz")
SWEEPS = 3
LOW, HIGH = 0.25, 2.0
ROUNDS = 9
WIDTHS = (1, 3, 3, 3, 3, 4, 3, 3, 3)
PAD = 8


def cheb_constants():
    mid, half = 0.5 * (HIGH + LOW), 0.5 * (HIGH - LOW)
    s = mid / half
    rho = 1.0 / s
    steps = []
    for _ in range(SWEEPS):
        nxt = 1.0 / (2.0 * s - rho)
        steps.append((nxt * rho, 2.0 * nxt / half))
        rho = nxt
    return mid, steps


def kernel(counts, chunks, eta_hbm, force_hbm, sol_hbm, res_hbm,
           e_ref, b_ref, f_ref, cxm_ref, cxp_ref, cym_ref, cyp_ref, czm_ref, czp_ref, dg_ref, inv_ref,
           r_ref, w0_ref, w1_ref, so_ref, ro_ref,
           sy_ref, hy_ref, sz_ref, hz_ref, ar_ref,
           in_sem, out_sem, xs_sem, xr_sem, ys_sem, yr_sem, zs_sem, zr_sem, as_sem, ar_sem):
    X, Y, Z = b_ref.shape[1:]
    mid, steps = cheb_constants()
    me = [lax.axis_index(a) for a in AXES]
    nch = len(chunks)
    order = [0] + ([nch - 1] if nch > 1 else []) + list(range(1, nch - 1))

    load_e = pltpu.make_async_copy(eta_hbm, e_ref.at[0, pl.ds(1, X), pl.ds(PAD, Y)], in_sem.at[0])
    load_b = pltpu.make_async_copy(force_hbm, b_ref, in_sem.at[1])
    load_e.start()
    load_b.start()

    def device(dim, index):
        spot = list(me)
        spot[dim] = index
        return tuple(spot)

    barrier = pltpu.get_barrier_semaphore()
    for dim in range(3):
        for off in range(1, counts[dim]):
            pl.semaphore_signal(barrier, inc=1, device_id=device(dim, lax.rem(me[dim] + off, counts[dim])),
                                device_id_type=MESH)

    def field(k):
        return e_ref if k == 0 else f_ref.at[k - 1]

    def target(dim, side):
        return device(dim, me[dim] + (1 if side == 0 else -1))

    def sends(dim, side):
        return me[dim] < counts[dim] - 1 if side == 0 else me[dim] > 0

    def receives(dim, side):
        return me[dim] > 0 if side == 0 else me[dim] < counts[dim] - 1

    def x_copy(k, side):
        n = WIDTHS[k]
        face, halo = (X, 0) if side == 0 else (1, X + 1)
        return pltpu.make_async_remote_copy(
            src_ref=field(k).at[pl.ds(0, n), face, pl.ds(PAD, Y)],
            dst_ref=field(k).at[pl.ds(0, n), halo, pl.ds(PAD, Y)],
            send_sem=xs_sem.at[k, side], recv_sem=xr_sem.at[k, side],
            device_id=target(0, side), device_id_type=MESH)

    def y_copy(k, side, ch):
        n = WIDTHS[k]
        lo, hi = chunks[ch]
        return pltpu.make_async_remote_copy(
            src_ref=sy_ref.at[k, side, pl.ds(0, n), pl.ds(lo, hi - lo)],
            dst_ref=hy_ref.at[k, side, pl.ds(0, n), pl.ds(lo, hi - lo)],
            send_sem=ys_sem.at[k, side, ch], recv_sem=yr_sem.at[k, side, ch],
            device_id=target(1, side), device_id_type=MESH)

    def z_copy(k, side, ch):
        return pltpu.make_async_remote_copy(
            src_ref=sz_ref.at[k, side, ch], dst_ref=hz_ref.at[k, side, ch],
            send_sem=zs_sem.at[k, side, ch], recv_sem=zr_sem.at[k, side, ch],
            device_id=target(2, side), device_id_type=MESH)

    def start_chunk(k, ch):
        for side in (0, 1):
            @pl.when(sends(1, side))
            def _():
                y_copy(k, side, ch).start()
            @pl.when(sends(2, side))
            def _():
                z_copy(k, side, ch).start()
        for side, edge in ((0, nch - 1), (1, 0)):
            if ch == edge:
                @pl.when(sends(0, side))
                def _():
                    x_copy(k, side).start()

    def wait_chunk(k, ch):
        for side in (0, 1):
            @pl.when(receives(1, side))
            def _():
                y_copy(k, side, ch).wait_recv()
            @pl.when(receives(2, side))
            def _():
                z_copy(k, side, ch).wait_recv()
        for side, edge in ((0, 0), (1, nch - 1)):
            if ch == edge:
                @pl.when(receives(0, side))
                def _():
                    x_copy(k, side).wait_recv()

    for side in (0, 1):
        @pl.when(jnp.logical_not(receives(0, side)))
        def _():
            zero = jnp.zeros((Y, Z), jnp.float32)
            for k in range(ROUNDS):
                for c in range(WIDTHS[k]):
                    field(k)[c, 0 if side == 0 else X + 1, PAD:PAD + Y] = zero
        @pl.when(jnp.logical_not(receives(1, side)))
        def _():
            def body(k, carry):
                hy_ref[k, side] = jnp.zeros(hy_ref.shape[2:], jnp.float32)
                return carry
            lax.fori_loop(0, ROUNDS, body, 0)
        @pl.when(jnp.logical_not(receives(2, side)))
        def _():
            def body(k, carry):
                hz_ref[k, side] = jnp.zeros(hz_ref.shape[2:], jnp.float32)
                return carry
            lax.fori_loop(0, ROUNDS, body, 0)

    lane = lax.broadcasted_iota(jnp.int32, (Y, Z), 1)
    blank = jnp.zeros((Y, Z), jnp.float32)
    first_lane, last_lane = lane == 0, lane == Z - 1

    def neighbours(k, ch, c, x):
        f = field(k)
        u = f[c, x + 1, PAD:PAD + Y]
        spot = c * X + x
        ym = f[c, x + 1, PAD - 1:PAD - 1 + Y]
        yp = f[c, x + 1, PAD + 1:PAD + 1 + Y]
        zm = jnp.where(first_lane, pltpu.roll(hz_ref[k, 0, ch], lax.rem(Z - spot, Z), 1), pltpu.roll(u, 1, 1))
        zp = jnp.where(last_lane, pltpu.roll(hz_ref[k, 1, ch], Z - 1 - spot, 1), pltpu.roll(u, Z - 1, 1))
        return u, f[c, x, PAD:PAD + Y], f[c, x + 2, PAD:PAD + Y], ym, yp, zm, zp

    def put(k, c, x, value, packs, store=True):
        if store:
            field(k)[c, x + 1, PAD:PAD + Y] = value
        sy_ref[k, 0, c, pl.ds(x, 1)] = value[Y - 1:Y]
        sy_ref[k, 1, c, pl.ds(x, 1)] = value[0:1]
        here = lane == c * X + x
        return (jnp.where(here, jnp.broadcast_to(value[:, Z - 1:Z], (Y, Z)), packs[0]),
                jnp.where(here, jnp.broadcast_to(value[:, 0:1], (Y, Z)), packs[1]))

    def sweep(need, make, body, extra=()):
        for ch in order:
            lo, hi = chunks[ch]
            if need is not None:
                wait_chunk(need, ch)
                def rim(x, carry):
                    for c in range(WIDTHS[need]):
                        field(need)[c, x + 1, PAD - 1:PAD] = hy_ref[need, 0, c, pl.ds(x, 1)]
                        field(need)[c, x + 1, PAD + Y:PAD + Y + 1] = hy_ref[need, 1, c, pl.ds(x, 1)]
                    return carry
                lax.fori_loop(lo, hi, rim, 0, unroll=hi - lo)
            def step(x, carry):
                return body(ch, x, carry[0], carry[1])
            packs, extra = lax.fori_loop(lo, hi, step, ((blank, blank), extra), unroll=hi - lo)
            if make is not None:
                sz_ref[make, 0, ch] = packs[0]
                sz_ref[make, 1, ch] = packs[1]
                start_chunk(make, ch)
        return extra

    load_e.wait()
    pl.semaphore_wait(barrier, sum(counts) - 3)
    sweep(None, 0, lambda ch, x, packs, extra: (put(0, 0, x, e_ref[0, x + 1, PAD:PAD + Y], packs, False), extra))
    load_b.wait()

    def setup(ch, x, packs, extra):
        u, xm, xp, ym, yp, zm, zp = neighbours(0, ch, 0, x)
        cxm, cxp = 0.5 * (u + xm), 0.5 * (u + xp)
        cym, cyp = 0.5 * (u + ym), 0.5 * (u + yp)
        czm, czp = 0.5 * (u + zm), 0.5 * (u + zp)
        diagonal = cxp + cxm + cyp + cym + czp + czm
        inverse = 1.0 / diagonal
        dg_ref[x] = diagonal
        inv_ref[x] = inverse
        cxm_ref[x], cxp_ref[x] = cxm * inverse, cxp * inverse
        cym_ref[x], cyp_ref[x] = cym * inverse, cyp * inverse
        czm_ref[x], czp_ref[x] = czm * inverse, czp * inverse
        for c in range(3):
            packs = put(1, c, x, b_ref[c, x] * inverse * (1.0 / mid), packs)
        return packs, extra

    sweep(0, 1, setup)

    def coefs(x):
        return (cxm_ref[x], cxp_ref[x], cym_ref[x], cyp_ref[x], czm_ref[x], czp_ref[x])

    def scaled(near, coef):
        u, xm, xp, ym, yp, zm, zp = near
        cxm, cxp, cym, cyp, czm, czp = coef
        return u - ((cxp * xp + cxm * xm) + (cyp * yp + cym * ym) + (czp * zp + czm * zm))

    def smooth(base, forcing, at, shift=None):
        keep, gain = steps[at]
        src, dst = base + at, base + at + 1
        last = at == SWEEPS - 1

        def body(ch, x, packs, extra):
            coef = coefs(x)
            inverse = inv_ref[x] if at == 0 else None
            for c in range(3):
                near = neighbours(src, ch, c, x)
                r = (forcing[c, x] * inverse if at == 0 else r_ref[c, x]) - scaled(near, coef)
                d = keep * near[0] + gain * r
                if last:
                    for k in range(base, dst):
                        d = d + (near[0] if k == src else field(k)[c, x + 1, PAD:PAD + Y])
                    if shift is not None:
                        d = d - shift * f_ref[base - 2, c, x + 1, PAD:PAD + Y]
                else:
                    r_ref[c, x] = r
                packs = put(dst, c, x, d, packs)
            return packs, extra

        sweep(src, dst, body)

    stages = (2, 0, 1)
    starts = [sum(counts[d] for d in stages[:i]) for i in range(3)]

    def ar_copy(which, stage, off):
        dim = stages[stage]
        slot = starts[stage] + me[dim]
        peer = lax.rem(me[dim] + off, counts[dim])
        return pltpu.make_async_remote_copy(
            src_ref=ar_ref.at[which, slot], dst_ref=ar_ref.at[which, slot],
            send_sem=as_sem.at[which, starts[stage] + off], recv_sem=ar_sem.at[which, slot],
            device_id=device(dim, peer), device_id_type=MESH)

    def ar_start(which, stage, tile):
        dim = stages[stage]
        ar_ref[which, starts[stage] + me[dim]] = tile
        for off in range(1, counts[dim]):
            ar_copy(which, stage, off).start()

    def ar_wait(which, stage):
        dim = stages[stage]
        for off in range(1, counts[dim]):
            slot = starts[stage] + lax.rem(me[dim] + off, counts[dim])
            pltpu.make_async_remote_copy(
                src_ref=ar_ref.at[which, slot], dst_ref=ar_ref.at[which, slot],
                send_sem=as_sem.at[which, starts[stage] + off], recv_sem=ar_sem.at[which, slot],
                device_id=device(dim, lax.rem(me[dim] + off, counts[dim])), device_id_type=MESH).wait_recv()
        total = ar_ref[which, starts[stage]]
        for i in range(1, counts[dim]):
            total = total + ar_ref[which, starts[stage] + i]
        return total

    rows8 = lax.broadcasted_iota(jnp.int32, (8, Z), 0)

    def tile_of(sums):
        tile = jnp.zeros((8, Z), jnp.float32)
        for i, s in enumerate(sums):
            tile = jnp.where(rows8 == i, jnp.sum(s, axis=0, keepdims=True), tile)
        return tile

    def totals(tile, n):
        whole = jnp.broadcast_to(jnp.sum(tile, axis=1, keepdims=True), (8, Z))
        return [whole[i:i + 1] for i in range(n)]

    for at in range(SWEEPS):
        smooth(1, b_ref, at)

    def stokes0(ch, x, packs, sums):
        bb, wb, ww = sums
        coef, diagonal = coefs(x), dg_ref[x]
        near = [neighbours(4, ch, c, x) for c in range(3)]
        for c in range(3):
            part, b = scaled(near[c], coef), b_ref[c, x]
            w = diagonal * part
            bb, wb, ww = bb + b * b, wb + w * b, ww + w * w
            w0_ref[c, x] = w
            packs = put(5, c, x, part * (1.0 / mid), packs)
        div = -0.5 * (near[0][2] - near[0][1] + (near[1][4] - near[1][3]) + (near[2][6] - near[2][5]))
        ww = ww + div * div
        w0_ref[3, x] = div
        packs = put(5, 3, x, e_ref[0, x + 1, PAD:PAD + Y] * div, packs)
        return packs, (bb, wb, ww)

    sums = sweep(4, 5, stokes0, (blank, blank, blank))
    ar_start(0, 0, tile_of(sums))

    smooth(5, w0_ref, 0)
    ar_start(0, 1, ar_wait(0, 0))
    smooth(5, w0_ref, 1)
    ar_start(0, 2, ar_wait(0, 1))
    square, wb, ww = totals(ar_wait(0, 2), 3)
    h00 = wb / square
    h10 = jnp.sqrt(ww / square - h00 * h00)
    smooth(5, w0_ref, 2, h00)

    def stokes1(ch, x, packs, sums):
        wb, wu, ww = sums
        coef, diagonal = coefs(x), dg_ref[x]
        near = [neighbours(8, ch, c, x) for c in range(3)]
        _, pxm, pxp, pym, pyp, pzm, pzp = neighbours(5, ch, 3, x)
        grads = (0.5 * (pxp - pxm), 0.5 * (pyp - pym), 0.5 * (pzp - pzm))
        for c in range(3):
            w, b = diagonal * scaled(near[c], coef) + grads[c], b_ref[c, x]
            u = w0_ref[c, x] - h00 * b
            wb, wu, ww = wb + w * b, wu + w * u, ww + w * w
            w1_ref[c, x] = w
        div = -0.5 * (near[0][2] - near[0][1] + (near[1][4] - near[1][3]) + (near[2][6] - near[2][5]))
        wu, ww = wu + div * w0_ref[3, x], ww + div * div
        w1_ref[3, x] = div
        return packs, (wb, wu, ww)

    sums = sweep(8, None, stokes1, (blank, blank, blank))
    ar_start(1, 0, tile_of(sums))
    ar_start(1, 1, ar_wait(1, 0))
    ar_start(1, 2, ar_wait(1, 1))
    wb, wu, ww = totals(ar_wait(1, 2), 3)

    beta = jnp.sqrt(square)
    h01 = wb / (square * h10)
    h11 = wu / (square * h10 * h10)
    h21 = jnp.sqrt(ww / (square * h10 * h10) - h01 * h01 - h11 * h11)
    n00, n01, n11 = h00 * h00 + h10 * h10, h00 * h01 + h10 * h11, h01 * h01 + h11 * h11 + h21 * h21
    l00 = jnp.sqrt(n00)
    l10 = n01 / l00
    l11 = jnp.sqrt(n11 - l10 * l10)
    g0 = beta * h00 / l00
    g1 = (beta * h01 - l10 * g0) / l11
    y1 = g1 / l11
    y0 = (g0 - l10 * y1) / l00
    c0 = beta - (h00 * y0 + h01 * y1)
    c1 = -(h10 * y0 + h11 * y1)
    c2 = -(h21 * y1)
    z0_weight, z1_weight = y0 / beta, y1 / (beta * h10)
    b_weight = (c0 - c2 * h01 / h21) / beta
    u_weight = (c1 - c2 * h11 / h21) / (beta * h10)
    w_weight = c2 / (h21 * beta * h10)

    def out_copies(ch):
        lo, hi = chunks[ch]
        span = pl.ds(lo, hi - lo)
        return (pltpu.make_async_copy(so_ref.at[:, span], sol_hbm.at[:, span], out_sem.at[0, ch]),
                pltpu.make_async_copy(ro_ref.at[:, span], res_hbm.at[:, span], out_sem.at[1, ch]))

    for ch in range(nch):
        def body(x, carry):
            for c in range(3):
                b = b_ref[c, x]
                so_ref[c, x] = z0_weight * f_ref[3, c, x + 1, PAD:PAD + Y] + z1_weight * f_ref[7, c, x + 1, PAD:PAD + Y]
                ro_ref[c, x] = b_weight * b + u_weight * (w0_ref[c, x] - h00 * b) + w_weight * w1_ref[c, x]
            so_ref[3, x] = z1_weight * f_ref[4, 3, x + 1, PAD:PAD + Y]
            ro_ref[3, x] = u_weight * w0_ref[3, x] + w_weight * w1_ref[3, x]
            return carry
        lax.fori_loop(*chunks[ch], body, 0, unroll=4)
        for copy in out_copies(ch):
            copy.start()

    for side in (0, 1):
        @pl.when(sends(0, side))
        def _():
            for k in range(ROUNDS):
                x_copy(k, side).wait_send()
        @pl.when(sends(1, side))
        def _():
            for k in range(ROUNDS):
                for ch in range(nch):
                    y_copy(k, side, ch).wait_send()
        @pl.when(sends(2, side))
        def _():
            for k in range(ROUNDS):
                for ch in range(nch):
                    z_copy(k, side, ch).wait_send()
    for which in (0, 1):
        for stage in range(3):
            for off in range(1, counts[stages[stage]]):
                ar_copy(which, stage, off).wait_send()
    for ch in range(nch):
        for copy in out_copies(ch):
            copy.wait()


def solution(mesh):
    counts = tuple(mesh.shape[a] for a in AXES)

    def shards(viscosity, force):
        X, Y, Z = viscosity.shape
        assert 4 * X <= Z
        size = 8 if X % 8 == 0 else X
        chunks = tuple((lo, lo + size) for lo in range(0, X, size))
        nch = len(chunks)
        f32 = jnp.float32
        block = pltpu.VMEM((X, Y, Z), f32)
        dma = pltpu.SemaphoreType.DMA
        spots = sum(counts)
        scratch = [
            pltpu.VMEM((1, X + 2, Y + 2 * PAD, Z), f32), pltpu.VMEM((3, X, Y, Z), f32),
            pltpu.VMEM((ROUNDS - 1, 4, X + 2, Y + 2 * PAD, Z), f32),
            block, block, block, block, block, block, block, block,
            pltpu.VMEM((3, X, Y, Z), f32),
            pltpu.VMEM((4, X, Y, Z), f32), pltpu.VMEM((4, X, Y, Z), f32),
            pltpu.VMEM((4, X, Y, Z), f32), pltpu.VMEM((4, X, Y, Z), f32),
            pltpu.VMEM((ROUNDS, 2, 4, X, Z), f32), pltpu.VMEM((ROUNDS, 2, 4, X, Z), f32),
            pltpu.VMEM((ROUNDS, 2, nch, Y, Z), f32), pltpu.VMEM((ROUNDS, 2, nch, Y, Z), f32),
            pltpu.VMEM((2, spots, 8, Z), f32),
            dma((2,)), dma((2, nch)), dma((ROUNDS, 2)), dma((ROUNDS, 2)),
            dma((ROUNDS, 2, nch)), dma((ROUNDS, 2, nch)), dma((ROUNDS, 2, nch)), dma((ROUNDS, 2, nch)),
            dma((2, spots)), dma((2, spots)),
        ]
        anywhere = pl.BlockSpec(memory_space=pl.ANY)
        out = jax.ShapeDtypeStruct((4, X, Y, Z), f32)
        return tuple(pl.pallas_call(
            functools.partial(kernel, counts, chunks),
            out_shape=(out, out),
            in_specs=[anywhere, anywhere],
            out_specs=(anywhere, anywhere),
            scratch_shapes=scratch,
            name="fgmres",
            compiler_params=pltpu.CompilerParams(
                collective_id=0, has_side_effects=True, vmem_limit_bytes=56 * 1024 * 1024),
        )(viscosity, force))

    return jax.shard_map(
        shards,
        mesh=mesh,
        in_specs=(P("gx", "gy", "gz"), P(None, "gx", "gy", "gz")),
        out_specs=(P(None, "gx", "gy", "gz"), P(None, "gx", "gy", "gz")),
        check_vma=False,
    )
```

```python
import functools
import jax
import jax.numpy as jnp
from jax import lax
from jax.experimental import pallas as pl
from jax.experimental.pallas import tpu as pltpu
from jax.sharding import PartitionSpec as P

MESH = pl.DeviceIdType.MESH
AXES = ("gx", "gy", "gz")
SWEEPS = 3
LOW, HIGH = 0.25, 2.0
ROUNDS = 9
WIDTHS = (1, 3, 3, 3, 3, 4, 3, 3, 3)
UNROLL = 4
PAD = 8


def cheb_constants():
    mid, half = 0.5 * (HIGH + LOW), 0.5 * (HIGH - LOW)
    s = mid / half
    rho = 1.0 / s
    steps = []
    for _ in range(SWEEPS):
        nxt = 1.0 / (2.0 * s - rho)
        steps.append((nxt * rho, 2.0 * nxt / half))
        rho = nxt
    return mid, steps


def kernel(counts, chunks, eta_hbm, force_hbm, sol_hbm, res_hbm,
           e_ref, b_ref, f_ref, cxm_ref, cxp_ref, cym_ref, cyp_ref, czm_ref, czp_ref, dg_ref, inv_ref,
           r_ref, w0_ref, w1_ref, so_ref, ro_ref,
           sy_ref, hy_ref, sz_ref, hz_ref, ar_ref,
           in_sem, out_sem, xs_sem, xr_sem, ys_sem, yr_sem, zs_sem, zr_sem, as_sem, ar_sem):
    X, Y, Z = b_ref.shape[1:]
    mid, steps = cheb_constants()
    me = [lax.axis_index(a) for a in AXES]
    size, nch = chunks

    load_e = pltpu.make_async_copy(eta_hbm, e_ref.at[0, pl.ds(1, X), pl.ds(PAD, Y)], in_sem.at[0])
    load_b = pltpu.make_async_copy(force_hbm, b_ref, in_sem.at[1])
    load_e.start()
    load_b.start()

    def device(dim, index):
        spot = list(me)
        spot[dim] = index
        return tuple(spot)

    barrier = pltpu.get_barrier_semaphore()
    for dim in range(3):
        for off in range(1, counts[dim]):
            pl.semaphore_signal(barrier, inc=1, device_id=device(dim, lax.rem(me[dim] + off, counts[dim])),
                                device_id_type=MESH)

    def field(k):
        return e_ref if k == 0 else f_ref.at[k - 1]

    def target(dim, side):
        return device(dim, me[dim] + (1 if side == 0 else -1))

    def sends(dim, side):
        return me[dim] < counts[dim] - 1 if side == 0 else me[dim] > 0

    def receives(dim, side):
        return me[dim] > 0 if side == 0 else me[dim] < counts[dim] - 1

    def x_copy(k, side):
        n = WIDTHS[k]
        face, halo = (X, 0) if side == 0 else (1, X + 1)
        return pltpu.make_async_remote_copy(
            src_ref=field(k).at[pl.ds(0, n), face, pl.ds(PAD, Y)],
            dst_ref=field(k).at[pl.ds(0, n), halo, pl.ds(PAD, Y)],
            send_sem=xs_sem.at[k, side], recv_sem=xr_sem.at[k, side],
            device_id=target(0, side), device_id_type=MESH)

    def y_copy(k, side, ch):
        n = WIDTHS[k]
        span = pl.ds(pl.multiple_of(ch * size, size), size)
        return pltpu.make_async_remote_copy(
            src_ref=sy_ref.at[k, side, pl.ds(0, n), span],
            dst_ref=hy_ref.at[k, side, pl.ds(0, n), span],
            send_sem=ys_sem.at[k, side, ch], recv_sem=yr_sem.at[k, side, ch],
            device_id=target(1, side), device_id_type=MESH)

    def z_copy(k, side, ch):
        return pltpu.make_async_remote_copy(
            src_ref=sz_ref.at[k, side, ch], dst_ref=hz_ref.at[k, side, ch],
            send_sem=zs_sem.at[k, side, ch], recv_sem=zr_sem.at[k, side, ch],
            device_id=target(2, side), device_id_type=MESH)

    def start_chunk(k, ch):
        for side in (0, 1):
            @pl.when(sends(1, side))
            def _():
                y_copy(k, side, ch).start()
            @pl.when(sends(2, side))
            def _():
                z_copy(k, side, ch).start()
        for side, edge in ((0, nch - 1), (1, 0)):
            @pl.when(jnp.logical_and(ch == edge, sends(0, side)))
            def _():
                x_copy(k, side).start()

    def wait_chunk(k, ch):
        for side in (0, 1):
            @pl.when(receives(1, side))
            def _():
                y_copy(k, side, ch).wait_recv()
            @pl.when(receives(2, side))
            def _():
                z_copy(k, side, ch).wait_recv()
        for side, edge in ((0, 0), (1, nch - 1)):
            @pl.when(jnp.logical_and(ch == edge, receives(0, side)))
            def _():
                x_copy(k, side).wait_recv()

    for side in (0, 1):
        @pl.when(jnp.logical_not(receives(0, side)))
        def _():
            zero = jnp.zeros((Y, Z), jnp.float32)
            for k in range(ROUNDS):
                for c in range(WIDTHS[k]):
                    field(k)[c, 0 if side == 0 else X + 1, PAD:PAD + Y] = zero
        @pl.when(jnp.logical_not(receives(1, side)))
        def _():
            def body(k, carry):
                hy_ref[k, side] = jnp.zeros(hy_ref.shape[2:], jnp.float32)
                return carry
            lax.fori_loop(0, ROUNDS, body, 0)
        @pl.when(jnp.logical_not(receives(2, side)))
        def _():
            def body(k, carry):
                hz_ref[k, side] = jnp.zeros(hz_ref.shape[2:], jnp.float32)
                return carry
            lax.fori_loop(0, ROUNDS, body, 0)

    lane = lax.broadcasted_iota(jnp.int32, (Y, Z), 1)
    blank = jnp.zeros((Y, Z), jnp.float32)
    first_lane, last_lane = lane == 0, lane == Z - 1

    def neighbours(k, ch, c, x):
        f = field(k)
        u = f[c, x + 1, PAD:PAD + Y]
        spot = c * X + x
        ym = f[c, x + 1, PAD - 1:PAD - 1 + Y]
        yp = f[c, x + 1, PAD + 1:PAD + 1 + Y]
        zm = jnp.where(first_lane, pltpu.roll(hz_ref[k, 0, ch], lax.rem(Z - spot, Z), 1), pltpu.roll(u, 1, 1))
        zp = jnp.where(last_lane, pltpu.roll(hz_ref[k, 1, ch], Z - 1 - spot, 1), pltpu.roll(u, Z - 1, 1))
        return u, f[c, x, PAD:PAD + Y], f[c, x + 2, PAD:PAD + Y], ym, yp, zm, zp

    def put(k, c, x, value, store=True):
        if store:
            field(k)[c, x + 1, PAD:PAD + Y] = value
        sy_ref[k, 0, c, pl.ds(x, 1)] = value[Y - 1:Y]
        sy_ref[k, 1, c, pl.ds(x, 1)] = value[0:1]

    def sweep(need, make, body, extra=()):
        def chunk(i, extra):
            ch = lax.rem(i * (nch - 1), nch)
            lo = pl.multiple_of(ch * size, size)
            if need is not None:
                wait_chunk(need, ch)
                for c in range(WIDTHS[need]):
                    low, high = hy_ref[need, 0, c, pl.ds(lo, size)], hy_ref[need, 1, c, pl.ds(lo, size)]
                    for j in range(size):
                        field(need)[c, lo + j + 1, PAD - 1:PAD] = low[j:j + 1]
                        field(need)[c, lo + j + 1, PAD + Y:PAD + Y + 1] = high[j:j + 1]
            extra = lax.fori_loop(0, size, lambda j, extra: body(ch, lo + j, extra), extra, unroll=UNROLL)
            if make is not None:
                low = high = blank
                for j in range(size):
                    for c in range(WIDTHS[make]):
                        spot = c * X + lo + j
                        here = lane == spot
                        value = field(make)[c, lo + j + 1, PAD:PAD + Y]
                        low = jnp.where(here, pltpu.roll(value, lax.rem(spot + 1, Z), 1), low)
                        high = jnp.where(here, pltpu.roll(value, spot, 1), high)
                sz_ref[make, 0, ch] = low
                sz_ref[make, 1, ch] = high
                start_chunk(make, ch)
            return extra
        return lax.fori_loop(0, nch, chunk, extra)

    load_e.wait()
    pl.semaphore_wait(barrier, sum(counts) - 3)
    def first(ch, x, extra):
        put(0, 0, x, e_ref[0, x + 1, PAD:PAD + Y], False)
        return extra

    sweep(None, 0, first)
    load_b.wait()

    def setup(ch, x, extra):
        u, xm, xp, ym, yp, zm, zp = neighbours(0, ch, 0, x)
        cxm, cxp = 0.5 * (u + xm), 0.5 * (u + xp)
        cym, cyp = 0.5 * (u + ym), 0.5 * (u + yp)
        czm, czp = 0.5 * (u + zm), 0.5 * (u + zp)
        diagonal = cxp + cxm + cyp + cym + czp + czm
        inverse = 1.0 / diagonal
        dg_ref[x] = diagonal
        inv_ref[x] = inverse
        cxm_ref[x], cxp_ref[x] = cxm * inverse, cxp * inverse
        cym_ref[x], cyp_ref[x] = cym * inverse, cyp * inverse
        czm_ref[x], czp_ref[x] = czm * inverse, czp * inverse
        for c in range(3):
            put(1, c, x, b_ref[c, x] * inverse * (1.0 / mid))
        return extra

    sweep(0, 1, setup)

    def coefs(x):
        return (cxm_ref[x], cxp_ref[x], cym_ref[x], cyp_ref[x], czm_ref[x], czp_ref[x])

    def scaled(near, coef):
        u, xm, xp, ym, yp, zm, zp = near
        cxm, cxp, cym, cyp, czm, czp = coef
        return u - ((cxp * xp + cxm * xm) + (cyp * yp + cym * ym) + (czp * zp + czm * zm))

    def smooth(base, forcing, at, shift=None):
        keep, gain = steps[at]
        src, dst = base + at, base + at + 1
        last = at == SWEEPS - 1

        def body(ch, x, extra):
            coef = coefs(x)
            inverse = inv_ref[x] if at == 0 else None
            for c in range(3):
                near = neighbours(src, ch, c, x)
                r = (forcing[c, x] * inverse if at == 0 else r_ref[c, x]) - scaled(near, coef)
                d = keep * near[0] + gain * r
                if last:
                    for k in range(base, dst):
                        d = d + (near[0] if k == src else field(k)[c, x + 1, PAD:PAD + Y])
                    if shift is not None:
                        d = d - shift * f_ref[base - 2, c, x + 1, PAD:PAD + Y]
                else:
                    r_ref[c, x] = r
                put(dst, c, x, d)
            return extra

        sweep(src, dst, body)

    stages = (2, 0, 1)
    starts = [sum(counts[d] for d in stages[:i]) for i in range(3)]

    def ar_copy(which, stage, off):
        dim = stages[stage]
        slot = starts[stage] + me[dim]
        peer = lax.rem(me[dim] + off, counts[dim])
        return pltpu.make_async_remote_copy(
            src_ref=ar_ref.at[which, slot], dst_ref=ar_ref.at[which, slot],
            send_sem=as_sem.at[which, starts[stage] + off], recv_sem=ar_sem.at[which, slot],
            device_id=device(dim, peer), device_id_type=MESH)

    def ar_start(which, stage, tile):
        dim = stages[stage]
        ar_ref[which, starts[stage] + me[dim]] = tile
        for off in range(1, counts[dim]):
            ar_copy(which, stage, off).start()

    def ar_wait(which, stage):
        dim = stages[stage]
        for off in range(1, counts[dim]):
            slot = starts[stage] + lax.rem(me[dim] + off, counts[dim])
            pltpu.make_async_remote_copy(
                src_ref=ar_ref.at[which, slot], dst_ref=ar_ref.at[which, slot],
                send_sem=as_sem.at[which, starts[stage] + off], recv_sem=ar_sem.at[which, slot],
                device_id=device(dim, lax.rem(me[dim] + off, counts[dim])), device_id_type=MESH).wait_recv()
        total = ar_ref[which, starts[stage]]
        for i in range(1, counts[dim]):
            total = total + ar_ref[which, starts[stage] + i]
        return total

    rows8 = lax.broadcasted_iota(jnp.int32, (8, Z), 0)

    def tile_of(sums):
        tile = jnp.zeros((8, Z), jnp.float32)
        for i, s in enumerate(sums):
            tile = jnp.where(rows8 == i, jnp.sum(s, axis=0, keepdims=True), tile)
        return tile

    def totals(tile, n):
        whole = jnp.broadcast_to(jnp.sum(tile, axis=1, keepdims=True), (8, Z))
        return [whole[i:i + 1] for i in range(n)]

    for at in range(SWEEPS):
        smooth(1, b_ref, at)

    def stokes0(ch, x, sums):
        bb, wb, ww = sums
        coef, diagonal = coefs(x), dg_ref[x]
        near = [neighbours(4, ch, c, x) for c in range(3)]
        for c in range(3):
            part, b = scaled(near[c], coef), b_ref[c, x]
            w = diagonal * part
            bb, wb, ww = bb + b * b, wb + w * b, ww + w * w
            w0_ref[c, x] = w
            put(5, c, x, part * (1.0 / mid))
        div = -0.5 * (near[0][2] - near[0][1] + (near[1][4] - near[1][3]) + (near[2][6] - near[2][5]))
        ww = ww + div * div
        w0_ref[3, x] = div
        put(5, 3, x, e_ref[0, x + 1, PAD:PAD + Y] * div)
        return (bb, wb, ww)

    sums = sweep(4, 5, stokes0, (blank, blank, blank))
    ar_start(0, 0, tile_of(sums))

    smooth(5, w0_ref, 0)
    ar_start(0, 1, ar_wait(0, 0))
    smooth(5, w0_ref, 1)
    ar_start(0, 2, ar_wait(0, 1))
    square, wb, ww = totals(ar_wait(0, 2), 3)
    h00 = wb / square
    h10 = jnp.sqrt(ww / square - h00 * h00)
    smooth(5, w0_ref, 2, h00)

    def stokes1(ch, x, sums):
        wb, wu, ww = sums
        coef, diagonal = coefs(x), dg_ref[x]
        near = [neighbours(8, ch, c, x) for c in range(3)]
        _, pxm, pxp, pym, pyp, pzm, pzp = neighbours(5, ch, 3, x)
        grads = (0.5 * (pxp - pxm), 0.5 * (pyp - pym), 0.5 * (pzp - pzm))
        for c in range(3):
            w, b = diagonal * scaled(near[c], coef) + grads[c], b_ref[c, x]
            u = w0_ref[c, x] - h00 * b
            wb, wu, ww = wb + w * b, wu + w * u, ww + w * w
            w1_ref[c, x] = w
        div = -0.5 * (near[0][2] - near[0][1] + (near[1][4] - near[1][3]) + (near[2][6] - near[2][5]))
        wu, ww = wu + div * w0_ref[3, x], ww + div * div
        w1_ref[3, x] = div
        return (wb, wu, ww)

    sums = sweep(8, None, stokes1, (blank, blank, blank))
    ar_start(1, 0, tile_of(sums))
    ar_start(1, 1, ar_wait(1, 0))
    ar_start(1, 2, ar_wait(1, 1))
    wb, wu, ww = totals(ar_wait(1, 2), 3)

    beta = jnp.sqrt(square)
    h01 = wb / (square * h10)
    h11 = wu / (square * h10 * h10)
    h21 = jnp.sqrt(ww / (square * h10 * h10) - h01 * h01 - h11 * h11)
    n00, n01, n11 = h00 * h00 + h10 * h10, h00 * h01 + h10 * h11, h01 * h01 + h11 * h11 + h21 * h21
    l00 = jnp.sqrt(n00)
    l10 = n01 / l00
    l11 = jnp.sqrt(n11 - l10 * l10)
    g0 = beta * h00 / l00
    g1 = (beta * h01 - l10 * g0) / l11
    y1 = g1 / l11
    y0 = (g0 - l10 * y1) / l00
    c0 = beta - (h00 * y0 + h01 * y1)
    c1 = -(h10 * y0 + h11 * y1)
    c2 = -(h21 * y1)
    z0_weight, z1_weight = y0 / beta, y1 / (beta * h10)
    b_weight = (c0 - c2 * h01 / h21) / beta
    u_weight = (c1 - c2 * h11 / h21) / (beta * h10)
    w_weight = c2 / (h21 * beta * h10)

    def out_copies(ch):
        span = pl.ds(ch * size, size)
        return (pltpu.make_async_copy(so_ref.at[:, span], sol_hbm.at[:, span], out_sem.at[0, ch]),
                pltpu.make_async_copy(ro_ref.at[:, span], res_hbm.at[:, span], out_sem.at[1, ch]))

    def finish(ch, carry):
        def body(j, carry):
            x = ch * size + j
            for c in range(3):
                b = b_ref[c, x]
                so_ref[c, x] = (z0_weight * f_ref[3, c, x + 1, PAD:PAD + Y]
                                + z1_weight * f_ref[7, c, x + 1, PAD:PAD + Y])
                ro_ref[c, x] = b_weight * b + u_weight * (w0_ref[c, x] - h00 * b) + w_weight * w1_ref[c, x]
            so_ref[3, x] = z1_weight * f_ref[4, 3, x + 1, PAD:PAD + Y]
            ro_ref[3, x] = u_weight * w0_ref[3, x] + w_weight * w1_ref[3, x]
            return carry
        lax.fori_loop(0, size, body, 0, unroll=UNROLL)
        for copy in out_copies(ch):
            copy.start()
        return carry

    lax.fori_loop(0, nch, finish, 0)

    def each_chunk(act):
        def body(ch, carry):
            act(ch)
            return carry
        lax.fori_loop(0, nch, body, 0)

    for side in (0, 1):
        @pl.when(sends(0, side))
        def _():
            for k in range(ROUNDS):
                x_copy(k, side).wait_send()
        @pl.when(sends(1, side))
        def _():
            for k in range(ROUNDS):
                each_chunk(lambda ch: y_copy(k, side, ch).wait_send())
        @pl.when(sends(2, side))
        def _():
            for k in range(ROUNDS):
                each_chunk(lambda ch: z_copy(k, side, ch).wait_send())
    for which in (0, 1):
        for stage in range(3):
            for off in range(1, counts[stages[stage]]):
                ar_copy(which, stage, off).wait_send()
    each_chunk(lambda ch: [copy.wait() for copy in out_copies(ch)])


def solution(mesh):
    counts = tuple(mesh.shape[a] for a in AXES)

    def shards(viscosity, force):
        X, Y, Z = viscosity.shape
        assert 4 * X <= Z
        size = 8 if X % 8 == 0 else X
        nch = X // size
        chunks = (size, nch)
        f32 = jnp.float32
        block = pltpu.VMEM((X, Y, Z), f32)
        dma = pltpu.SemaphoreType.DMA
        spots = sum(counts)
        scratch = [
            pltpu.VMEM((1, X + 2, Y + 2 * PAD, Z), f32), pltpu.VMEM((3, X, Y, Z), f32),
            pltpu.VMEM((ROUNDS - 1, 4, X + 2, Y + 2 * PAD, Z), f32),
            block, block, block, block, block, block, block, block,
            pltpu.VMEM((3, X, Y, Z), f32),
            pltpu.VMEM((4, X, Y, Z), f32), pltpu.VMEM((4, X, Y, Z), f32),
            pltpu.VMEM((4, X, Y, Z), f32), pltpu.VMEM((4, X, Y, Z), f32),
            pltpu.VMEM((ROUNDS, 2, 4, X, Z), f32), pltpu.VMEM((ROUNDS, 2, 4, X, Z), f32),
            pltpu.VMEM((ROUNDS, 2, nch, Y, Z), f32), pltpu.VMEM((ROUNDS, 2, nch, Y, Z), f32),
            pltpu.VMEM((2, spots, 8, Z), f32),
            dma((2,)), dma((2, nch)), dma((ROUNDS, 2)), dma((ROUNDS, 2)),
            dma((ROUNDS, 2, nch)), dma((ROUNDS, 2, nch)), dma((ROUNDS, 2, nch)), dma((ROUNDS, 2, nch)),
            dma((2, spots)), dma((2, spots)),
        ]
        anywhere = pl.BlockSpec(memory_space=pl.ANY)
        out = jax.ShapeDtypeStruct((4, X, Y, Z), f32)
        return tuple(pl.pallas_call(
            functools.partial(kernel, counts, chunks),
            out_shape=(out, out),
            in_specs=[anywhere, anywhere],
            out_specs=(anywhere, anywhere),
            scratch_shapes=scratch,
            name="fgmres",
            compiler_params=pltpu.CompilerParams(
                collective_id=0, has_side_effects=True, vmem_limit_bytes=56 * 1024 * 1024),
        )(viscosity, force))

    return jax.shard_map(
        shards,
        mesh=mesh,
        in_specs=(P("gx", "gy", "gz"), P(None, "gx", "gy", "gz")),
        out_specs=(P(None, "gx", "gy", "gz"), P(None, "gx", "gy", "gz")),
        check_vma=False,
    )
```

```python
import functools
import jax
import jax.numpy as jnp
from jax import lax
from jax.experimental import pallas as pl
from jax.experimental.pallas import tpu as pltpu
from jax.sharding import PartitionSpec as P

MESH = pl.DeviceIdType.MESH
AXES = ("gx", "gy", "gz")
SWEEPS = 3
LOW, HIGH = 0.25, 2.0
ROUNDS = 9
WIDTHS = (1, 3, 3, 3, 3, 4, 3, 3, 3)
UNROLL = 8
PAD = 8


def cheb_constants():
    mid, half = 0.5 * (HIGH + LOW), 0.5 * (HIGH - LOW)
    s = mid / half
    rho = 1.0 / s
    steps = []
    for _ in range(SWEEPS):
        nxt = 1.0 / (2.0 * s - rho)
        steps.append((nxt * rho, 2.0 * nxt / half))
        rho = nxt
    return mid, steps


def kernel(counts, chunks, eta_hbm, force_hbm, sol_hbm, res_hbm,
           e_ref, b_ref, f_ref, cxm_ref, cxp_ref, cym_ref, cyp_ref, czm_ref, czp_ref, dg_ref, inv_ref,
           r_ref, w0_ref, w1_ref, so_ref, ro_ref,
           sy_ref, hy_ref, sz_ref, hz_ref, ar_ref,
           in_sem, out_sem, xs_sem, xr_sem, ys_sem, yr_sem, zs_sem, zr_sem, as_sem, ar_sem):
    X, Y, Z = b_ref.shape[1:]
    mid, steps = cheb_constants()
    me = [lax.axis_index(a) for a in AXES]
    size, nch = chunks

    load_e = pltpu.make_async_copy(eta_hbm, e_ref.at[0, pl.ds(1, X), pl.ds(PAD, Y)], in_sem.at[0])
    load_b = pltpu.make_async_copy(force_hbm, b_ref, in_sem.at[1])
    load_e.start()
    load_b.start()

    def device(dim, index):
        spot = list(me)
        spot[dim] = index
        return tuple(spot)

    barrier = pltpu.get_barrier_semaphore()
    for dim in range(3):
        for off in range(1, counts[dim]):
            pl.semaphore_signal(barrier, inc=1, device_id=device(dim, lax.rem(me[dim] + off, counts[dim])),
                                device_id_type=MESH)

    def field(k):
        return e_ref if k == 0 else f_ref.at[k - 1]

    def target(dim, side):
        return device(dim, me[dim] + (1 if side == 0 else -1))

    def sends(dim, side):
        return me[dim] < counts[dim] - 1 if side == 0 else me[dim] > 0

    def receives(dim, side):
        return me[dim] > 0 if side == 0 else me[dim] < counts[dim] - 1

    def x_copy(k, side):
        n = WIDTHS[k]
        face, halo = (X, 0) if side == 0 else (1, X + 1)
        return pltpu.make_async_remote_copy(
            src_ref=field(k).at[pl.ds(0, n), face, pl.ds(PAD, Y)],
            dst_ref=field(k).at[pl.ds(0, n), halo, pl.ds(PAD, Y)],
            send_sem=xs_sem.at[k, side], recv_sem=xr_sem.at[k, side],
            device_id=target(0, side), device_id_type=MESH)

    def y_copy(k, side, ch):
        n = WIDTHS[k]
        span = pl.ds(pl.multiple_of(ch * size, size), size)
        return pltpu.make_async_remote_copy(
            src_ref=sy_ref.at[k, side, pl.ds(0, n), span],
            dst_ref=hy_ref.at[k, side, pl.ds(0, n), span],
            send_sem=ys_sem.at[k, side, ch], recv_sem=yr_sem.at[k, side, ch],
            device_id=target(1, side), device_id_type=MESH)

    def z_copy(k, side, ch):
        return pltpu.make_async_remote_copy(
            src_ref=sz_ref.at[k, side, ch], dst_ref=hz_ref.at[k, side, ch],
            send_sem=zs_sem.at[k, side, ch], recv_sem=zr_sem.at[k, side, ch],
            device_id=target(2, side), device_id_type=MESH)

    def start_chunk(k, ch):
        for side in (0, 1):
            @pl.when(sends(1, side))
            def _():
                y_copy(k, side, ch).start()
            @pl.when(sends(2, side))
            def _():
                z_copy(k, side, ch).start()
        for side, edge in ((0, nch - 1), (1, 0)):
            @pl.when(jnp.logical_and(ch == edge, sends(0, side)))
            def _():
                x_copy(k, side).start()

    def wait_chunk(k, ch):
        for side in (0, 1):
            @pl.when(receives(1, side))
            def _():
                y_copy(k, side, ch).wait_recv()
            @pl.when(receives(2, side))
            def _():
                z_copy(k, side, ch).wait_recv()
        for side, edge in ((0, 0), (1, nch - 1)):
            @pl.when(jnp.logical_and(ch == edge, receives(0, side)))
            def _():
                x_copy(k, side).wait_recv()

    for side in (0, 1):
        @pl.when(jnp.logical_not(receives(0, side)))
        def _():
            zero = jnp.zeros((Y, Z), jnp.float32)
            for k in range(ROUNDS):
                for c in range(WIDTHS[k]):
                    field(k)[c, 0 if side == 0 else X + 1, PAD:PAD + Y] = zero
        @pl.when(jnp.logical_not(receives(1, side)))
        def _():
            def body(k, carry):
                hy_ref[k, side] = jnp.zeros(hy_ref.shape[2:], jnp.float32)
                return carry
            lax.fori_loop(0, ROUNDS, body, 0)
        @pl.when(jnp.logical_not(receives(2, side)))
        def _():
            def body(k, carry):
                hz_ref[k, side] = jnp.zeros(hz_ref.shape[2:], jnp.float32)
                return carry
            lax.fori_loop(0, ROUNDS, body, 0)

    lane = lax.broadcasted_iota(jnp.int32, (Y, Z), 1)
    blank = jnp.zeros((Y, Z), jnp.float32)
    first_lane, last_lane = lane == 0, lane == Z - 1

    def neighbours(k, ch, c, x):
        f = field(k)
        u = f[c, x + 1, PAD:PAD + Y]
        spot = c * X + x
        ym = f[c, x + 1, PAD - 1:PAD - 1 + Y]
        yp = f[c, x + 1, PAD + 1:PAD + 1 + Y]
        zm = jnp.where(first_lane, pltpu.roll(hz_ref[k, 0, ch], lax.rem(Z - spot, Z), 1), pltpu.roll(u, 1, 1))
        zp = jnp.where(last_lane, pltpu.roll(hz_ref[k, 1, ch], Z - 1 - spot, 1), pltpu.roll(u, Z - 1, 1))
        return u, f[c, x, PAD:PAD + Y], f[c, x + 2, PAD:PAD + Y], ym, yp, zm, zp

    def put(k, c, x, value, store=True):
        if store:
            field(k)[c, x + 1, PAD:PAD + Y] = value
        sy_ref[k, 0, c, pl.ds(x, 1)] = value[Y - 1:Y]
        sy_ref[k, 1, c, pl.ds(x, 1)] = value[0:1]

    def sweep(need, make, body, extra=()):
        def chunk(i, extra):
            ch = lax.rem(i * (nch - 1), nch)
            lo = pl.multiple_of(ch * size, size)
            if need is not None:
                wait_chunk(need, ch)
                for c in range(WIDTHS[need]):
                    low, high = hy_ref[need, 0, c, pl.ds(lo, size)], hy_ref[need, 1, c, pl.ds(lo, size)]
                    for j in range(size):
                        field(need)[c, lo + j + 1, PAD - 1:PAD] = low[j:j + 1]
                        field(need)[c, lo + j + 1, PAD + Y:PAD + Y + 1] = high[j:j + 1]
            extra = lax.fori_loop(0, size, lambda j, extra: body(ch, lo + j, extra), extra, unroll=UNROLL)
            if make is not None:
                low = high = blank
                for j in range(size):
                    for c in range(WIDTHS[make]):
                        spot = c * X + lo + j
                        here = lane == spot
                        value = field(make)[c, lo + j + 1, PAD:PAD + Y]
                        low = jnp.where(here, pltpu.roll(value, lax.rem(spot + 1, Z), 1), low)
                        high = jnp.where(here, pltpu.roll(value, spot, 1), high)
                sz_ref[make, 0, ch] = low
                sz_ref[make, 1, ch] = high
                start_chunk(make, ch)
            return extra
        return lax.fori_loop(0, nch, chunk, extra)

    load_e.wait()
    pl.semaphore_wait(barrier, sum(counts) - 3)
    def first(ch, x, extra):
        put(0, 0, x, e_ref[0, x + 1, PAD:PAD + Y], False)
        return extra

    sweep(None, 0, first)
    load_b.wait()

    def setup(ch, x, extra):
        u, xm, xp, ym, yp, zm, zp = neighbours(0, ch, 0, x)
        cxm, cxp = 0.5 * (u + xm), 0.5 * (u + xp)
        cym, cyp = 0.5 * (u + ym), 0.5 * (u + yp)
        czm, czp = 0.5 * (u + zm), 0.5 * (u + zp)
        diagonal = cxp + cxm + cyp + cym + czp + czm
        inverse = 1.0 / diagonal
        dg_ref[x] = diagonal
        inv_ref[x] = inverse
        cxm_ref[x], cxp_ref[x] = cxm * inverse, cxp * inverse
        cym_ref[x], cyp_ref[x] = cym * inverse, cyp * inverse
        czm_ref[x], czp_ref[x] = czm * inverse, czp * inverse
        for c in range(3):
            put(1, c, x, b_ref[c, x] * inverse * (1.0 / mid))
        return extra

    sweep(0, 1, setup)

    def coefs(x):
        return (cxm_ref[x], cxp_ref[x], cym_ref[x], cyp_ref[x], czm_ref[x], czp_ref[x])

    def scaled(near, coef):
        u, xm, xp, ym, yp, zm, zp = near
        cxm, cxp, cym, cyp, czm, czp = coef
        return u - ((cxp * xp + cxm * xm) + (cyp * yp + cym * ym) + (czp * zp + czm * zm))

    def smooth(base, forcing, at, shift=None):
        keep, gain = steps[at]
        src, dst = base + at, base + at + 1
        last = at == SWEEPS - 1

        def body(ch, x, extra):
            coef = coefs(x)
            inverse = inv_ref[x] if at == 0 else None
            for c in range(3):
                near = neighbours(src, ch, c, x)
                r = (forcing[c, x] * inverse if at == 0 else r_ref[c, x]) - scaled(near, coef)
                d = keep * near[0] + gain * r
                if last:
                    for k in range(base, dst):
                        d = d + (near[0] if k == src else field(k)[c, x + 1, PAD:PAD + Y])
                    if shift is not None:
                        d = d - shift * f_ref[base - 2, c, x + 1, PAD:PAD + Y]
                else:
                    r_ref[c, x] = r
                put(dst, c, x, d)
            return extra

        sweep(src, dst, body)

    stages = (2, 0, 1)
    starts = [sum(counts[d] for d in stages[:i]) for i in range(3)]

    def ar_copy(which, stage, off):
        dim = stages[stage]
        slot = starts[stage] + me[dim]
        peer = lax.rem(me[dim] + off, counts[dim])
        return pltpu.make_async_remote_copy(
            src_ref=ar_ref.at[which, slot], dst_ref=ar_ref.at[which, slot],
            send_sem=as_sem.at[which, starts[stage] + off], recv_sem=ar_sem.at[which, slot],
            device_id=device(dim, peer), device_id_type=MESH)

    def ar_start(which, stage, tile):
        dim = stages[stage]
        ar_ref[which, starts[stage] + me[dim]] = tile
        for off in range(1, counts[dim]):
            ar_copy(which, stage, off).start()

    def ar_wait(which, stage):
        dim = stages[stage]
        for off in range(1, counts[dim]):
            slot = starts[stage] + lax.rem(me[dim] + off, counts[dim])
            pltpu.make_async_remote_copy(
                src_ref=ar_ref.at[which, slot], dst_ref=ar_ref.at[which, slot],
                send_sem=as_sem.at[which, starts[stage] + off], recv_sem=ar_sem.at[which, slot],
                device_id=device(dim, lax.rem(me[dim] + off, counts[dim])), device_id_type=MESH).wait_recv()
        total = ar_ref[which, starts[stage]]
        for i in range(1, counts[dim]):
            total = total + ar_ref[which, starts[stage] + i]
        return total

    rows8 = lax.broadcasted_iota(jnp.int32, (8, Z), 0)

    def tile_of(sums):
        tile = jnp.zeros((8, Z), jnp.float32)
        for i, s in enumerate(sums):
            tile = jnp.where(rows8 == i, jnp.sum(s, axis=0, keepdims=True), tile)
        return tile

    def totals(tile, n):
        whole = jnp.broadcast_to(jnp.sum(tile, axis=1, keepdims=True), (8, Z))
        return [whole[i:i + 1] for i in range(n)]

    for at in range(SWEEPS):
        smooth(1, b_ref, at)

    def stokes0(ch, x, sums):
        bb, wb, ww = sums
        coef, diagonal = coefs(x), dg_ref[x]
        near = [neighbours(4, ch, c, x) for c in range(3)]
        for c in range(3):
            part, b = scaled(near[c], coef), b_ref[c, x]
            w = diagonal * part
            bb, wb, ww = bb + b * b, wb + w * b, ww + w * w
            w0_ref[c, x] = w
            put(5, c, x, part * (1.0 / mid))
        div = -0.5 * (near[0][2] - near[0][1] + (near[1][4] - near[1][3]) + (near[2][6] - near[2][5]))
        ww = ww + div * div
        w0_ref[3, x] = div
        put(5, 3, x, e_ref[0, x + 1, PAD:PAD + Y] * div)
        return (bb, wb, ww)

    sums = sweep(4, 5, stokes0, (blank, blank, blank))
    ar_start(0, 0, tile_of(sums))

    smooth(5, w0_ref, 0)
    ar_start(0, 1, ar_wait(0, 0))
    smooth(5, w0_ref, 1)
    ar_start(0, 2, ar_wait(0, 1))
    square, wb, ww = totals(ar_wait(0, 2), 3)
    h00 = wb / square
    h10 = jnp.sqrt(ww / square - h00 * h00)
    smooth(5, w0_ref, 2, h00)

    def stokes1(ch, x, sums):
        wb, wu, ww = sums
        coef, diagonal = coefs(x), dg_ref[x]
        near = [neighbours(8, ch, c, x) for c in range(3)]
        _, pxm, pxp, pym, pyp, pzm, pzp = neighbours(5, ch, 3, x)
        grads = (0.5 * (pxp - pxm), 0.5 * (pyp - pym), 0.5 * (pzp - pzm))
        for c in range(3):
            w, b = diagonal * scaled(near[c], coef) + grads[c], b_ref[c, x]
            u = w0_ref[c, x] - h00 * b
            wb, wu, ww = wb + w * b, wu + w * u, ww + w * w
            w1_ref[c, x] = w
        div = -0.5 * (near[0][2] - near[0][1] + (near[1][4] - near[1][3]) + (near[2][6] - near[2][5]))
        wu, ww = wu + div * w0_ref[3, x], ww + div * div
        w1_ref[3, x] = div
        return (wb, wu, ww)

    sums = sweep(8, None, stokes1, (blank, blank, blank))
    ar_start(1, 0, tile_of(sums))
    ar_start(1, 1, ar_wait(1, 0))
    ar_start(1, 2, ar_wait(1, 1))
    wb, wu, ww = totals(ar_wait(1, 2), 3)

    beta = jnp.sqrt(square)
    h01 = wb / (square * h10)
    h11 = wu / (square * h10 * h10)
    h21 = jnp.sqrt(ww / (square * h10 * h10) - h01 * h01 - h11 * h11)
    n00, n01, n11 = h00 * h00 + h10 * h10, h00 * h01 + h10 * h11, h01 * h01 + h11 * h11 + h21 * h21
    l00 = jnp.sqrt(n00)
    l10 = n01 / l00
    l11 = jnp.sqrt(n11 - l10 * l10)
    g0 = beta * h00 / l00
    g1 = (beta * h01 - l10 * g0) / l11
    y1 = g1 / l11
    y0 = (g0 - l10 * y1) / l00
    c0 = beta - (h00 * y0 + h01 * y1)
    c1 = -(h10 * y0 + h11 * y1)
    c2 = -(h21 * y1)
    z0_weight, z1_weight = y0 / beta, y1 / (beta * h10)
    b_weight = (c0 - c2 * h01 / h21) / beta
    u_weight = (c1 - c2 * h11 / h21) / (beta * h10)
    w_weight = c2 / (h21 * beta * h10)

    def out_copies(ch):
        span = pl.ds(ch * size, size)
        return (pltpu.make_async_copy(so_ref.at[:, span], sol_hbm.at[:, span], out_sem.at[0, ch]),
                pltpu.make_async_copy(ro_ref.at[:, span], res_hbm.at[:, span], out_sem.at[1, ch]))

    def finish(ch, carry):
        def body(j, carry):
            x = ch * size + j
            for c in range(3):
                b = b_ref[c, x]
                so_ref[c, x] = (z0_weight * f_ref[3, c, x + 1, PAD:PAD + Y]
                                + z1_weight * f_ref[7, c, x + 1, PAD:PAD + Y])
                ro_ref[c, x] = b_weight * b + u_weight * (w0_ref[c, x] - h00 * b) + w_weight * w1_ref[c, x]
            so_ref[3, x] = z1_weight * f_ref[4, 3, x + 1, PAD:PAD + Y]
            ro_ref[3, x] = u_weight * w0_ref[3, x] + w_weight * w1_ref[3, x]
            return carry
        lax.fori_loop(0, size, body, 0, unroll=UNROLL)
        for copy in out_copies(ch):
            copy.start()
        return carry

    lax.fori_loop(0, nch, finish, 0)

    def each_chunk(act):
        def body(ch, carry):
            act(ch)
            return carry
        lax.fori_loop(0, nch, body, 0)

    for side in (0, 1):
        @pl.when(sends(0, side))
        def _():
            for k in range(ROUNDS):
                x_copy(k, side).wait_send()
        @pl.when(sends(1, side))
        def _():
            for k in range(ROUNDS):
                each_chunk(lambda ch: y_copy(k, side, ch).wait_send())
        @pl.when(sends(2, side))
        def _():
            for k in range(ROUNDS):
                each_chunk(lambda ch: z_copy(k, side, ch).wait_send())
    for which in (0, 1):
        for stage in range(3):
            for off in range(1, counts[stages[stage]]):
                ar_copy(which, stage, off).wait_send()
    each_chunk(lambda ch: [copy.wait() for copy in out_copies(ch)])


def solution(mesh):
    counts = tuple(mesh.shape[a] for a in AXES)

    def shards(viscosity, force):
        X, Y, Z = viscosity.shape
        assert 4 * X <= Z
        size = 8 if X % 8 == 0 else X
        nch = X // size
        chunks = (size, nch)
        f32 = jnp.float32
        block = pltpu.VMEM((X, Y, Z), f32)
        dma = pltpu.SemaphoreType.DMA
        spots = sum(counts)
        scratch = [
            pltpu.VMEM((1, X + 2, Y + 2 * PAD, Z), f32), pltpu.VMEM((3, X, Y, Z), f32),
            pltpu.VMEM((ROUNDS - 1, 4, X + 2, Y + 2 * PAD, Z), f32),
            block, block, block, block, block, block, block, block,
            pltpu.VMEM((3, X, Y, Z), f32),
            pltpu.VMEM((4, X, Y, Z), f32), pltpu.VMEM((4, X, Y, Z), f32),
            pltpu.VMEM((4, X, Y, Z), f32), pltpu.VMEM((4, X, Y, Z), f32),
            pltpu.VMEM((ROUNDS, 2, 4, X, Z), f32), pltpu.VMEM((ROUNDS, 2, 4, X, Z), f32),
            pltpu.VMEM((ROUNDS, 2, nch, Y, Z), f32), pltpu.VMEM((ROUNDS, 2, nch, Y, Z), f32),
            pltpu.VMEM((2, spots, 8, Z), f32),
            dma((2,)), dma((2, nch)), dma((ROUNDS, 2)), dma((ROUNDS, 2)),
            dma((ROUNDS, 2, nch)), dma((ROUNDS, 2, nch)), dma((ROUNDS, 2, nch)), dma((ROUNDS, 2, nch)),
            dma((2, spots)), dma((2, spots)),
        ]
        anywhere = pl.BlockSpec(memory_space=pl.ANY)
        out = jax.ShapeDtypeStruct((4, X, Y, Z), f32)
        return tuple(pl.pallas_call(
            functools.partial(kernel, counts, chunks),
            out_shape=(out, out),
            in_specs=[anywhere, anywhere],
            out_specs=(anywhere, anywhere),
            scratch_shapes=scratch,
            name="fgmres",
            compiler_params=pltpu.CompilerParams(
                collective_id=0, has_side_effects=True, vmem_limit_bytes=56 * 1024 * 1024),
        )(viscosity, force))

    return jax.shard_map(
        shards,
        mesh=mesh,
        in_specs=(P("gx", "gy", "gz"), P(None, "gx", "gy", "gz")),
        out_specs=(P(None, "gx", "gy", "gz"), P(None, "gx", "gy", "gz")),
        check_vma=False,
    )
```
